32 devices in a mesh: tm: 8 (over y, x, core), space: 4 (over z).
Axes of the slice: x: 2, y: 2, z: 4, core: 2. Of those that a mesh axis runs over, the one named last changes fastest.
Arguments:
- guess: float32 [32, 128, 4096], P('tm', 'space'), may hold values from -6 to 6
- forcing: float32 [32, 128, 4096], P('tm', 'space'), may hold values from -4 to 4
- initial: float32 [128, 4096], P('space'), may hold values from -6 to 6
- courant_rows: float32 [128, 4096], P('space'), may hold values from -0.12 to 0.12
- courant_cols: float32 [128, 4096], P('space'), may hold values from -0.12 to 0.12
- diffusion: float32 [128, 4096], P('space'), may hold values from 0.03 to 0.06
Outputs:
- states: float32 [32, 128, 4096], P('tm', 'space')
The draws below stay inside these ranges and needn't reach their ends.
All inputs are finite; a program needn't handle non-finite values.
Results may differ from the reference program's by a relative error of at most 0.00002.
Values sent between devices are 32-bit elements; how exact they have to be, the bound alone decides.
A program may use at most 64 MiB of HBM per device.

```python
import jax
import jax.numpy as jnp

COLS = 4096
STEPS_DEV = 4
ROWS = 128
NSTEPS = 32


def draw_courant_rows(key, part):
    magnitude = jax.random.uniform(jax.random.fold_in(key, 11), (ROWS, COLS), jnp.float32, 0.06, 0.12)
    return magnitude


def draw_diffusion(key, part):
    exponent = jax.random.uniform(jax.random.fold_in(key, 23), (ROWS, COLS), jnp.float32, jnp.log(0.03), jnp.log(0.06))
    return jnp.clip(jnp.exp(exponent), 0.03, 0.06)


def levels(key, extent, split, least, largest):
    def one(dim, shards_of):
        steps = jax.random.uniform(jax.random.fold_in(jax.random.fold_in(key, 6), dim), (shards_of,), jnp.float32, least / len(split), largest / len(split))
        return jnp.repeat(jnp.exp(steps), extent[dim] // shards_of).reshape((-1,) + (1,) * (len(extent) - dim - 1))

    level = one(*split[0])
    for cut in split[1:]:
        level = level * one(*cut)
    return level


def normal_values(own_key, extent, scale, bound, pieces=(), kind=jnp.bfloat16):
    entries = scale * jax.random.normal(own_key, extent, jnp.float32)
    if pieces:
        entries = entries * levels(own_key, extent, pieces, -0.22, 0.18)
    return jnp.clip(entries, -bound, bound).astype(kind)


def setup_inputs(seed: int = 0) -> dict:
    arg_keys = jax.random.split(jax.random.key(seed), 7)
    guess = normal_values(arg_keys[0], (NSTEPS, ROWS, COLS), 1.0, 6.0, ((0, 8), (1, 4)), jnp.float32)
    forcing = normal_values(arg_keys[1], (NSTEPS, ROWS, COLS), 0.5, 4.0, ((0, 8), (1, 4)), jnp.float32)
    initial = normal_values(arg_keys[2], (ROWS, COLS), 1.0, 6.0, ((0, 4),), jnp.float32)
    courant_rows = draw_courant_rows(jax.random.fold_in(arg_keys[6], 71), 0)
    courant_cols = jnp.clip(jax.random.uniform(arg_keys[4], (ROWS, COLS), jnp.float32, -0.12, 0.12) * levels(arg_keys[4], (ROWS, COLS), ((0, 4),), -0.4, 0.0), -0.12, 0.12)
    diffusion = draw_diffusion(jax.random.fold_in(arg_keys[6], 71), 0)
    return {"guess": guess, "forcing": forcing, "initial": initial, "courant_rows": courant_rows, "courant_cols": courant_cols, "diffusion": diffusion}


def stencil(field, rate_rows, rate_cols, spread):
    padded = jnp.pad(field, ((1, 1), (0, 0)))
    upper = padded[:-2]
    lower = padded[2:]
    left = jnp.roll(field, 1, axis=1)
    right = jnp.roll(field, -1, axis=1)
    advect = jnp.maximum(rate_rows, 0.0) * (field - upper) + jnp.minimum(rate_rows, 0.0) * (lower - field)
    advect = advect + jnp.maximum(rate_cols, 0.0) * (field - left) + jnp.minimum(rate_cols, 0.0) * (right - field)
    laplace = upper + lower + left + right - 4.0 * field
    return field - advect + spread * laplace


def reference(guess, forcing, initial, courant_rows, courant_cols, diffusion):
    steps_dev = STEPS_DEV
    count = guess.shape[0] // steps_dev
    guess_blocks = guess.reshape(count, steps_dev, guess.shape[1], guess.shape[2])
    force_blocks = forcing.reshape(count, steps_dev, guess.shape[1], guess.shape[2])
    residuals = []
    for block in range(count):
        current = initial if block == 0 else guess_blocks[block - 1, steps_dev - 1]
        for inner in range(steps_dev):
            current = stencil(current, courant_rows, courant_cols, diffusion) + force_blocks[block, inner]
        residuals.append(current - guess_blocks[block, steps_dev - 1])
    correction = jnp.zeros_like(initial)
    corrected = []
    for block in range(count):
        for inner in range(steps_dev // 2):
            correction = stencil(correction, 2.0 * courant_rows, 2.0 * courant_cols, 2.0 * diffusion)
        correction = correction + residuals[block]
        corrected.append(guess_blocks[block, steps_dev - 1] + correction)
    outputs = []
    for block in range(count):
        current = initial if block == 0 else corrected[block - 1]
        for inner in range(steps_dev - 1):
            current = stencil(current, courant_rows, courant_cols, diffusion) + force_blocks[block, inner]
            outputs.append(current)
        outputs.append(corrected[block])
    return jnp.stack(outputs)
```

```python
import functools

import jax
import jax.numpy as jnp
from jax import lax
from jax.experimental import pallas as pl
from jax.experimental.pallas import tpu as pltpu
from jax.sharding import PartitionSpec as P

TILE = 8
LANES = 128
MESH = pl.DeviceIdType.MESH


def packing(depth):
    items = [(("f", j), depth - 1 - j) for j in range(depth - 1)]
    items += [(("c", j), depth - 1) for j in range(3)]
    items = sorted(items, key=lambda item: -item[1])
    used, placed = [], []
    for source, rows in items:
        for tile in range(len(used) + 1):
            if tile == len(used):
                used.append(0)
            if used[tile] + rows <= TILE:
                placed.append((source, rows, tile, used[tile]))
                used[tile] += rows
                break
    return placed, len(used)


def rolled(value, shift, axis):
    shift = shift % value.shape[axis]
    return pltpu.roll(value, shift, axis) if shift else value


def step(u, coef):
    cu, cd, cl, cr, c0 = coef
    return (
        (c0 * u + cu * rolled(u, 1, 0))
        + (cd * rolled(u, -1, 0) + cl * rolled(u, 1, 1))
        + cr * rolled(u, -1, 1)
    )


def kernel(
    tcount, scount, chunks, depth, height, width,
    guess, forcing, initial, crow, ccol, diff, out,
    prev, own, frc, raw, pks, pkr, coef, ein, eout, res, ost,
    ldsem, psend, precv, isend, ksend, krecv, esend, erecv, osem,
):
    t = lax.axis_index("tm")
    s = lax.axis_index("space")
    span = width // chunks
    total = height + 2 * TILE
    placed, _ = packing(depth)
    mid = slice(TILE, TILE + height)
    up_ok, down_ok = s > 0, s < scount - 1
    first, not_first, not_last = t == 0, t > 0, t < tcount - 1

    def cols(c):
        return pl.ds(pl.multiple_of(c * span, LANES), span)

    def window(load, c):
        left = pl.ds(pl.multiple_of(lax.rem(c * span + width - LANES, width), LANES), LANES)
        right = pl.ds(pl.multiple_of(lax.rem((c + 1) * span, width), LANES), LANES)
        return jnp.concatenate([load(left), load(cols(c)), load(right)], axis=1)

    def remote(src, dst, ssem, rsem, dt, ds):
        return pltpu.make_async_remote_copy(
            src_ref=src, dst_ref=dst, send_sem=ssem, recv_sem=rsem,
            device_id=(t + dt, s + ds), device_id_type=MESH,
        )

    loads = [pltpu.make_async_copy(guess.at[depth - 1], own, ldsem.at[0])]
    for j in range(depth):
        loads.append(pltpu.make_async_copy(forcing.at[j], frc.at[j, mid], ldsem.at[1 + j]))
    for j, ref in enumerate((crow, ccol, diff)):
        loads.append(pltpu.make_async_copy(ref, raw.at[j], ldsem.at[1 + depth + j]))
    init_load = pltpu.make_async_copy(initial, prev.at[mid], ldsem.at[4 + depth])
    for load in loads:
        load.start()
    pl.when(first)(init_load.start)

    barrier = pltpu.get_barrier_semaphore()
    count = 0
    for dt in (-1, 0, 1):
        for ds in (-1, 0, 1):
            if dt == 0 and ds == 0:
                continue
            ok = (t + dt >= 0) & (t + dt < tcount) & (s + ds >= 0) & (s + ds < scount)

            @pl.when(ok)
            def _(dt=dt, ds=ds):
                pl.semaphore_signal(barrier, inc=1, device_id=(t + dt, s + ds), device_id_type=MESH)

            count = count + ok.astype(jnp.int32)

    @pl.when(s == 0)
    def _():
        prev[0:TILE] = jnp.zeros((TILE, width), jnp.float32)
        ein[0:TILE] = jnp.zeros((TILE, width), jnp.float32)
        pkr[0] = jnp.zeros(pkr.shape[1:], jnp.float32)

    @pl.when(s == scount - 1)
    def _():
        prev[TILE + height:] = jnp.zeros((TILE, width), jnp.float32)
        ein[TILE + height:] = jnp.zeros((TILE, width), jnp.float32)
        pkr[1] = jnp.zeros(pkr.shape[1:], jnp.float32)

    @pl.when(first)
    def _():
        ein[...] = jnp.zeros((total, width), jnp.float32)

    for load in loads:
        load.wait()
    pl.when(first)(init_load.wait)
    pl.semaphore_wait(barrier, count)

    top_rows, bottom_rows = slice(0, TILE), slice(height - TILE, height)
    top_halo, bottom_halo = slice(0, TILE), slice(TILE + height, total)

    def prev_copies(c):
        last = guess.at[depth - 1]
        return (
            (not_last, remote(last.at[:, cols(c)], prev.at[mid, cols(c)],
                              psend.at[0, c], precv.at[0, c], 1, 0)),
            (not_last & down_ok, remote(last.at[bottom_rows, cols(c)], prev.at[top_halo, cols(c)],
                                        psend.at[1, c], precv.at[1, c], 1, 1)),
            (not_last & up_ok, remote(last.at[top_rows, cols(c)], prev.at[bottom_halo, cols(c)],
                                      psend.at[2, c], precv.at[2, c], 1, -1)),
            (first & down_ok, remote(initial.at[bottom_rows, cols(c)], prev.at[top_halo, cols(c)],
                                     isend.at[0, c], precv.at[1, c], 0, 1)),
            (first & up_ok, remote(initial.at[top_rows, cols(c)], prev.at[bottom_halo, cols(c)],
                                   isend.at[1, c], precv.at[2, c], 0, -1)),
        )

    def pack_copies(c):
        return (
            (down_ok, remote(pks.at[0, :, cols(c)], pkr.at[0, :, cols(c)],
                             ksend.at[0, c], krecv.at[0, c], 0, 1)),
            (up_ok, remote(pks.at[1, :, cols(c)], pkr.at[1, :, cols(c)],
                           ksend.at[1, c], krecv.at[1, c], 0, -1)),
        )

    def e_copies(c):
        return (
            (not_last, remote(eout.at[:, cols(c)], ein.at[mid, cols(c)],
                              esend.at[0, c], erecv.at[0, c], 1, 0)),
            (not_last & down_ok, remote(eout.at[bottom_rows, cols(c)], ein.at[top_halo, cols(c)],
                                        esend.at[1, c], erecv.at[1, c], 1, 1)),
            (not_last & up_ok, remote(eout.at[top_rows, cols(c)], ein.at[bottom_halo, cols(c)],
                                      esend.at[2, c], erecv.at[2, c], 1, -1)),
        )

    row = lax.broadcasted_iota(jnp.int32, (TILE, span), 0)

    def source_rows(source, rows, c):
        kind, j = source
        if kind == "f":
            return frc[j, slice(TILE + rows.start, TILE + rows.stop), cols(c)]
        return raw[j, rows, cols(c)]

    def send_start(i, carry):
        c = lax.rem(t - 1 + i + chunks, chunks)
        tiles = [[None, None] for _ in range(pks.shape[1] // TILE)]
        for source, rows, tile, offset in placed:
            low = rolled(source_rows(source, bottom_rows, c), -offset, 0)
            high = rolled(source_rows(source, top_rows, c), offset, 0)
            if tiles[tile][0] is None:
                tiles[tile] = [low, high]
            else:
                tiles[tile][0] = jnp.where(row < TILE - offset, low, tiles[tile][0])
                tiles[tile][1] = jnp.where(row >= offset, high, tiles[tile][1])
        for tile, (low, high) in enumerate(tiles):
            pks[0, tile * TILE:(tile + 1) * TILE, cols(c)] = low
            pks[1, tile * TILE:(tile + 1) * TILE, cols(c)] = high
        for ok, copy in pack_copies(c) + prev_copies(lax.rem(t + i, chunks))[:3] + prev_copies(c)[3:]:
            pl.when(ok)(copy.start)
        return carry

    lax.fori_loop(0, chunks, send_start, 0)

    def wait_recv(sem_row, dst):
        return pltpu.make_async_copy(dst, dst, sem_row)

    def prepare(i):
        c = lax.rem(t - 1 + i + chunks, chunks)
        pl.when(not_first)(wait_recv(precv.at[0, c], prev.at[mid, cols(c)]).wait)

        @pl.when(up_ok)
        def _():
            wait_recv(precv.at[1, c], prev.at[top_halo, cols(c)]).wait()
            wait_recv(krecv.at[0, c], pkr.at[0, :, cols(c)]).wait()

        @pl.when(down_ok)
        def _():
            wait_recv(precv.at[2, c], prev.at[bottom_halo, cols(c)]).wait()
            wait_recv(krecv.at[1, c], pkr.at[1, :, cols(c)]).wait()

        ext = [None, None, None]
        for (kind, j), rows, tile, offset in placed:
            part = slice(tile * TILE, (tile + 1) * TILE)
            top = rolled(pkr[0, part, cols(c)], offset, 0)
            bottom = rolled(pkr[1, part, cols(c)], -offset, 0)
            if kind == "f":
                frc[j, top_halo, cols(c)] = top
                frc[j, bottom_halo, cols(c)] = bottom
            else:
                ext[j] = jnp.concatenate([top, raw[j, :, cols(c)], bottom], axis=0)
        a, b, d = ext
        cu = jnp.maximum(a, 0.0) + d
        cd = d - jnp.minimum(a, 0.0)
        cl = jnp.maximum(b, 0.0) + d
        cr = d - jnp.minimum(b, 0.0)
        coef[0, :, cols(c)] = cu
        coef[1, :, cols(c)] = cd
        coef[2, :, cols(c)] = cl
        coef[3, :, cols(c)] = cr
        coef[4, :, cols(c)] = 1.0 - ((cu + cd) + (cl + cr))

    def coef_of(c):
        return [window(lambda lanes, n=n: coef[n, :, lanes], c) for n in range(5)]

    def relax(i):
        c = lax.rem(t + i, chunks)
        cs = coef_of(c)
        u = window(lambda lanes: prev[:, lanes], c)
        for j in range(depth):
            u = step(u, cs)
            if j < depth - 1:
                u = u + window(lambda lanes: frc[j, :, lanes], c)
        w = u[mid, LANES:LANES + span] + frc[depth - 1, mid, cols(c)]
        res[:, cols(c)] = w - own[:, cols(c)]

    def coarse(i):
        c = lax.rem(t + i, chunks)
        cs = coef_of(c)
        u = window(lambda lanes: ein[:, lanes], c)
        for _ in range(depth // 2):
            u = 2.0 * step(u, cs) - u
        e = u[mid, LANES:LANES + span] + res[:, cols(c)]
        eout[:, cols(c)] = e
        ost[depth - 1, :, cols(c)] = own[:, cols(c)] + e
        for ok, copy in e_copies(c):
            pl.when(ok)(copy.start)

    def out_copy(c):
        return pltpu.make_async_copy(ost.at[:, :, cols(c)], out.at[:, :, cols(c)], osem.at[c])

    def final(i):
        c = lax.rem(t + i, chunks)
        cs = coef_of(c)
        u = window(lambda lanes: prev[:, lanes] + ein[:, lanes], c)
        for j in range(depth - 1):
            u = step(u, cs) + window(lambda lanes: frc[j, :, lanes], c)
            ost[j, :, cols(c)] = u[mid, LANES:LANES + span]
        out_copy(c).start()

    def wait_e(i):
        c = lax.rem(t - 1 + i + chunks, chunks)

        @pl.when(not_first)
        def _():
            wait_recv(erecv.at[0, c], ein.at[mid, cols(c)]).wait()

        @pl.when(not_first & up_ok)
        def _():
            wait_recv(erecv.at[1, c], ein.at[top_halo, cols(c)]).wait()

        @pl.when(not_first & down_ok)
        def _():
            wait_recv(erecv.at[2, c], ein.at[bottom_halo, cols(c)]).wait()

    for i in range(3):
        prepare(i)
    relax(0)
    wait_e(0)
    wait_e(1)

    def sweep(i, carry):
        @pl.when(i + 2 < chunks)
        def _():
            wait_e(i + 2)

        coarse(i)

        @pl.when(i + 3 < chunks)
        def _():
            prepare(i + 3)

        @pl.when(i + 1 < chunks)
        def _():
            relax(i + 1)

        final(i)
        return carry

    lax.fori_loop(0, chunks, sweep, 0)

    def finish(c, carry):
        for ok, copy in prev_copies(c) + pack_copies(c) + e_copies(c):
            pl.when(ok)(copy.wait_send)
        out_copy(c).wait()
        return carry

    lax.fori_loop(0, chunks, finish, 0)


def on_device(tcount, scount, guess, forcing, initial, crow, ccol, diff):
    depth, height, width = guess.shape
    chunks = max(n for n in (4, 8) if width % (n * LANES) == 0)
    _, tiles = packing(depth)
    total = height + 2 * TILE
    f32 = jnp.float32
    dma = pltpu.SemaphoreType.DMA
    return pl.pallas_call(
        functools.partial(kernel, tcount, scount, chunks, depth, height, width),
        out_shape=jax.ShapeDtypeStruct(guess.shape, f32),
        in_specs=[pl.BlockSpec(memory_space=pl.ANY)] * 6,
        out_specs=pl.BlockSpec(memory_space=pl.ANY),
        scratch_shapes=[
            pltpu.VMEM((total, width), f32),
            pltpu.VMEM((height, width), f32),
            pltpu.VMEM((depth, total, width), f32),
            pltpu.VMEM((3, height, width), f32),
            pltpu.VMEM((2, tiles * TILE, width), f32),
            pltpu.VMEM((2, tiles * TILE, width), f32),
            pltpu.VMEM((5, total, width), f32),
            pltpu.VMEM((total, width), f32),
            pltpu.VMEM((height, width), f32),
            pltpu.VMEM((height, width), f32),
            pltpu.VMEM((depth, height, width), f32),
            dma((5 + depth,)),
            dma((3, chunks)),
            dma((3, chunks)),
            dma((2, chunks)),
            dma((2, chunks)),
            dma((2, chunks)),
            dma((3, chunks)),
            dma((3, chunks)),
            dma((chunks,)),
        ],
        compiler_params=pltpu.CompilerParams(
            collective_id=0, has_side_effects=True, vmem_limit_bytes=48 << 20
        ),
    )(guess, forcing, initial, crow, ccol, diff)


def solution(mesh):
    return jax.shard_map(
        functools.partial(on_device, mesh.shape["tm"], mesh.shape["space"]),
        mesh=mesh,
        in_specs=(
            P("tm", "space", None),
            P("tm", "space", None),
            P("space", None),
            P("space", None),
            P("space", None),
            P("space", None),
        ),
        out_specs=P("tm", "space", None),
        check_vma=False,
    )
```

```python
import functools

import jax
import jax.numpy as jnp
from jax import lax
from jax.experimental import pallas as pl
from jax.experimental.pallas import tpu as pltpu
from jax.sharding import PartitionSpec as P

SUB = 8
LANES = 128
PIECE = 2
BLOCK = 2
MESH = pl.DeviceIdType.MESH


def shifted(x):
    lane = lax.broadcasted_iota(jnp.int32, x.shape[:2] + (LANES,), 2)
    size = x.shape[2]
    left = pltpu.roll(x, 1, 2)
    edge = left[:, :, :LANES]
    edge = jnp.where(lane == 0, pltpu.roll(edge, 1, 1), edge)
    left = jnp.concatenate([edge, left[:, :, LANES:]], axis=2)
    right = pltpu.roll(x, size - 1, 2)
    edge = right[:, :, size - LANES:]
    edge = jnp.where(lane == LANES - 1, pltpu.roll(edge, SUB - 1, 1), edge)
    right = jnp.concatenate([right[:, :, : size - LANES], edge], axis=2)
    return left, right


def kernel(
    tcount, scount, depth, height, lanes, nstart,
    guess, forcing, initial, crow, ccol, diff, out,
    prev, own, frc, raw, coef, ein, eout, res, ost, wa, wb,
    ldsem, ssend, srecv, esend, erecv, osem,
):
    t = lax.axis_index("tm")
    s = lax.axis_index("space")
    base = depth
    total = height + 2 * depth
    pieces = height // (2 * PIECE)
    up_ok, down_ok = s > 0, s < scount - 1
    first, not_first, not_last = t == 0, t > 0, t < tcount - 1
    field = pl.ds(base, height)

    def remote(src, dst, ssem, rsem, dt, ds):
        return pltpu.make_async_remote_copy(
            src_ref=src, dst_ref=dst, send_sem=ssem, recv_sem=rsem,
            device_id=(t + dt, s + ds), device_id_type=MESH,
        )

    loads = [pltpu.make_async_copy(guess, own, ldsem.at[0])]
    for j in range(depth):
        loads.append(pltpu.make_async_copy(forcing.at[j], frc.at[j, field], ldsem.at[1 + j]))
    for j, ref in enumerate((crow, ccol, diff)):
        loads.append(pltpu.make_async_copy(ref, raw.at[j, field], ldsem.at[1 + depth + j]))
    init_load = pltpu.make_async_copy(initial, prev.at[field], ldsem.at[4 + depth])
    for load in loads:
        load.start()
    pl.when(first)(init_load.start)

    barrier = pltpu.get_barrier_semaphore()
    count = 0
    for dt in (-1, 0, 1):
        for ds in (-1, 0, 1):
            if dt == 0 and ds == 0:
                continue
            ok = (t + dt >= 0) & (t + dt < tcount) & (s + ds >= 0) & (s + ds < scount)

            @pl.when(ok)
            def _(dt=dt, ds=ds):
                pl.semaphore_signal(barrier, inc=1, device_id=(t + dt, s + ds), device_id_type=MESH)

            count = count + ok.astype(jnp.int32)

    def clear(rows):
        zero = jnp.zeros((rows.size, SUB, lanes), jnp.float32)
        prev[rows] = zero
        ein[rows] = zero
        for j in range(depth - 1):
            frc[j, rows] = zero
        for j in range(3):
            raw[j, rows] = zero

    @pl.when(s == 0)
    def _():
        clear(pl.ds(0, depth))

    @pl.when(s == scount - 1)
    def _():
        clear(pl.ds(base + height, depth))

    @pl.when(first)
    def _():
        def body(i, carry):
            ein[i] = jnp.zeros((SUB, lanes), jnp.float32)
            return carry

        lax.fori_loop(0, total, body, 0)

    pl.semaphore_wait(barrier, count)

    starts = []

    def add(send_ok, src, dst, dt, ds, recv_ok, slot=None):
        n = len(starts)
        starts.append((send_ok, remote(src, dst, ssend.at[n], srecv.at[n if slot is None else slot], dt, ds), recv_ok))
        return n

    def halos(send_ok, src, dst, rows, dt, recv_ok, slots=(None, None)):
        low = add(send_ok & down_ok, src.at[pl.ds(height - rows, rows)], dst.at[pl.ds(base - rows, rows)],
                  dt, 1, None if recv_ok is None else recv_ok & up_ok, slots[0])
        high = add(send_ok & up_ok, src.at[pl.ds(0, rows)], dst.at[pl.ds(base + height, rows)],
                   dt, -1, None if recv_ok is None else recv_ok & down_ok, slots[1])
        return low, high

    always = t >= 0
    slots = halos(not_last, guess, prev, depth, 1, always)
    halos(first, initial, prev, depth, 0, None, slots)
    for j, ref in enumerate((crow, ccol, diff)):
        halos(always, ref, raw.at[j], depth - 1, 0, always)
    for j in range(depth - 1):
        halos(always, forcing.at[j], frc.at[j], depth - 1 - j, 0, always)
    add(not_last, guess, prev.at[field], 1, 0, not_first)
    assert len(starts) == nstart
    for ok, copy, _ in starts:
        pl.when(ok)(copy.start)
    for load in loads:
        load.wait()
    pl.when(first)(init_load.wait)
    for _, copy, ok in starts:
        if ok is not None:
            pl.when(ok)(copy.wait_recv)

    def coefficients(i, carry):
        row = i + 1
        a, b, d = raw[0, row], raw[1, row], raw[2, row]
        cu = jnp.maximum(a, 0.0) + d
        cd = d - jnp.minimum(a, 0.0)
        cl = jnp.maximum(b, 0.0) + d
        cr = d - jnp.minimum(b, 0.0)
        coef[0, row] = cu
        coef[1, row] = cd
        coef[2, row] = cl
        coef[3, row] = cr
        coef[4, row] = 1.0 - ((cu + cd) + (cl + cr))
        return carry

    lax.fori_loop(0, height + 2 * depth - 2, coefficients, 0)

    def step(ext, row, count):
        rows = pl.ds(row, count)
        u = ext[1:-1]
        left, right = shifted(u)
        return (
            (coef[4, rows] * u + coef[0, rows] * ext[:-2])
            + (coef[1, rows] * ext[2:] + coef[2, rows] * left)
            + coef[3, rows] * right
        )

    def sweep(src, margin, finish):
        low = base - margin

        def body(i, carry):
            row = low + i * BLOCK
            finish(row, step(src[pl.ds(row - 1, BLOCK + 2)], row, BLOCK))
            return carry

        lax.fori_loop(0, (height + 2 * margin) // BLOCK, body, 0)

    def advance(src, dst, j, margin, keep=False):
        def finish(row, value):
            value = value + frc[j, pl.ds(row, BLOCK)]
            dst[pl.ds(row, BLOCK)] = value

        sweep(src, margin, finish)

    buffers = (wa, wb)
    src = prev
    for j in range(depth - 1):
        advance(src, buffers[j % 2], j, depth - 1 - j)
        src = buffers[j % 2]

    def residual(row, value):
        rows = pl.ds(row - base, BLOCK)
        res[rows] = value + frc[depth - 1, pl.ds(row, BLOCK)] - own[rows]

    sweep(src, 0, residual)

    halo = depth - 1

    def e_copies(i):
        low, high = i * PIECE, height - (i + 1) * PIECE
        copies = [
            (not_last, not_first, remote(eout.at[pl.ds(row, PIECE)], ein.at[pl.ds(base + row, PIECE)],
                                         esend.at[side, i], erecv.at[side, i], 1, 0))
            for side, row in ((0, low), (1, high))
        ]
        rows = min(halo - low, PIECE)
        if rows > 0:
            copies.append((not_last & up_ok, not_first & down_ok, remote(
                eout.at[pl.ds(low, rows)], ein.at[pl.ds(base + height + low, rows)],
                esend.at[2, i], erecv.at[2, i], 1, -1)))
            copies.append((not_last & down_ok, not_first & up_ok, remote(
                eout.at[pl.ds(height - low - rows, rows)], ein.at[pl.ds(base - low - rows, rows)],
                esend.at[3, i], erecv.at[3, i], 1, 1)))
        return copies

    def wait_e(i):
        for _, ok, copy in e_copies(i):
            pl.when(ok)(copy.wait_recv)

    def coarse(row):
        reach = depth // 2
        x = ein[pl.ds(base + row - reach, PIECE + 2 * reach)]
        for k in range(reach):
            size = x.shape[0] - 2
            x = 2.0 * step(x, base + row - reach + k + 1, size) - x[1:-1]
        rows = pl.ds(row, PIECE)
        e = x + res[rows]
        eout[rows] = e
        ost[depth - 1, rows] = own[rows] + e

    def out_copy(j):
        return pltpu.make_async_copy(ost.at[j], out.at[j], osem.at[j])

    wait_e(0)
    for i in range(pieces):
        if i + 1 < pieces:
            wait_e(i + 1)
        coarse(i * PIECE)
        coarse(height - (i + 1) * PIECE)
        for ok, _, copy in e_copies(i):
            pl.when(ok)(copy.start)
    out_copy(depth - 1).start()

    def corrected(i, carry):
        wb[i + 1] = prev[i + 1] + ein[i + 1]
        return carry

    lax.fori_loop(0, total - 2, corrected, 0)
    src = wb
    for j in range(depth - 1):
        dst = buffers[j % 2]
        margin = depth - 2 - j

        def finish(row, value, j=j, dst=dst):
            dst[pl.ds(row, BLOCK)] = value + frc[j, pl.ds(row, BLOCK)]

        sweep(src, margin, finish)

        def stage(i, carry, j=j, dst=dst):
            ost[j, i] = dst[base + i]
            return carry

        lax.fori_loop(0, height, stage, 0)
        src = dst
        out_copy(j).start()

    for ok, copy, _ in starts:
        pl.when(ok)(copy.wait_send)
    for i in range(pieces):
        for ok, _, copy in e_copies(i):
            pl.when(ok)(copy.wait_send)
    for j in range(depth):
        out_copy(j).wait()


def on_device(tcount, scount, guess, forcing, initial, crow, ccol, diff):
    depth, height, width = guess.shape
    lanes = width // SUB
    assert lanes % LANES == 0 and height % (2 * PIECE) == 0
    total = height + 2 * depth
    nstart = 2 * (2 + 3 + depth - 1) + 1
    f32 = jnp.float32
    dma = pltpu.SemaphoreType.DMA

    def rows_of(value):
        return value.reshape(value.shape[:-1] + (SUB, lanes))

    def buffer(*dims):
        return pltpu.VMEM(dims + (SUB, lanes), f32)

    states = pl.pallas_call(
        functools.partial(kernel, tcount, scount, depth, height, lanes, nstart),
        out_shape=jax.ShapeDtypeStruct((depth, height, SUB, lanes), f32),
        in_specs=[pl.BlockSpec(memory_space=pl.ANY)] * 6,
        out_specs=pl.BlockSpec(memory_space=pl.ANY),
        scratch_shapes=[
            buffer(total),
            buffer(height),
            buffer(depth, total),
            buffer(3, total),
            buffer(5, total),
            buffer(total),
            buffer(height),
            buffer(height),
            buffer(depth, height),
            buffer(total),
            buffer(total),
            dma((5 + depth,)),
            dma((nstart,)),
            dma((nstart,)),
            dma((4, height // (2 * PIECE))),
            dma((4, height // (2 * PIECE))),
            dma((depth,)),
        ],
        compiler_params=pltpu.CompilerParams(
            collective_id=0, has_side_effects=True, vmem_limit_bytes=40 << 20
        ),
    )(*map(rows_of, (guess[depth - 1], forcing, initial, crow, ccol, diff)))
    return states.reshape(guess.shape)


def solution(mesh):
    return jax.shard_map(
        functools.partial(on_device, mesh.shape["tm"], mesh.shape["space"]),
        mesh=mesh,
        in_specs=(
            P("tm", "space", None),
            P("tm", "space", None),
            P("space", None),
            P("space", None),
            P("space", None),
            P("space", None),
        ),
        out_specs=P("tm", "space", None),
        check_vma=False,
    )
```

```python
import functools

import jax
import jax.numpy as jnp
from jax import lax
from jax.experimental import pallas as pl
from jax.experimental.pallas import tpu as pltpu
from jax.sharding import PartitionSpec as P

SUB = 8
LANES = 128
PIECE = 2
FLIGHT = 2
BLOCK = 2
MESH = pl.DeviceIdType.MESH


def shifted(x):
    lane = lax.broadcasted_iota(jnp.int32, x.shape[:2] + (LANES,), 2)
    size = x.shape[2]
    left = pltpu.roll(x, 1, 2)
    edge = left[:, :, :LANES]
    edge = jnp.where(lane == 0, pltpu.roll(edge, 1, 1), edge)
    left = jnp.concatenate([edge, left[:, :, LANES:]], axis=2)
    right = pltpu.roll(x, size - 1, 2)
    edge = right[:, :, size - LANES:]
    edge = jnp.where(lane == LANES - 1, pltpu.roll(edge, SUB - 1, 1), edge)
    right = jnp.concatenate([right[:, :, : size - LANES], edge], axis=2)
    return left, right


def kernel(
    tcount, scount, depth, height, lanes, nstart,
    guess, forcing, initial, crow, ccol, diff, out,
    prev, frc, raw, coef, ein, eout, res, wa, wb,
    ssend, srecv, esend, erecv,
):
    t = lax.axis_index("tm")
    s = lax.axis_index("space")
    base = depth
    total = height + 2 * depth
    pieces = height // (2 * PIECE)
    up_ok, down_ok = s > 0, s < scount - 1
    first, not_first, not_last = t == 0, t > 0, t < tcount - 1
    field = pl.ds(base, height)

    def remote(src, dst, ssem, rsem, dt, ds):
        return pltpu.make_async_remote_copy(
            src_ref=src, dst_ref=dst, send_sem=ssem, recv_sem=rsem,
            device_id=(t + dt, s + ds), device_id_type=MESH,
        )

    barrier = pltpu.get_barrier_semaphore()
    count = 0
    for dt in (-1, 0, 1):
        for ds in (-1, 0, 1):
            if dt == 0 and ds == 0:
                continue
            ok = (t + dt >= 0) & (t + dt < tcount) & (s + ds >= 0) & (s + ds < scount)

            @pl.when(ok)
            def _(dt=dt, ds=ds):
                pl.semaphore_signal(barrier, inc=1, device_id=(t + dt, s + ds), device_id_type=MESH)

            count = count + ok.astype(jnp.int32)

    def clear(rows):
        zero = jnp.zeros((rows.size, SUB, lanes), jnp.float32)
        prev[rows] = zero
        ein[rows] = zero
        for j in range(depth - 1):
            frc[j, rows] = zero
        for j in range(3):
            raw[j, rows] = zero

    @pl.when(s == 0)
    def _():
        clear(pl.ds(0, depth))

    @pl.when(s == scount - 1)
    def _():
        clear(pl.ds(base + height, depth))

    @pl.when(first)
    def _():
        def body(i, carry):
            ein[i] = jnp.zeros((SUB, lanes), jnp.float32)
            return carry

        lax.fori_loop(0, total, body, 0)

    pl.semaphore_wait(barrier, count)

    starts = []

    def add(send_ok, src, dst, dt, ds, recv_ok, slot=None):
        n = len(starts)
        starts.append((send_ok, remote(src, dst, ssend.at[n], srecv.at[n if slot is None else slot], dt, ds), recv_ok))
        return n

    def halos(send_ok, src, dst, rows, dt, recv_ok, slots=(None, None)):
        low = add(send_ok & down_ok, src.at[pl.ds(height - rows, rows)], dst.at[pl.ds(base - rows, rows)],
                  dt, 1, None if recv_ok is None else recv_ok & up_ok, slots[0])
        high = add(send_ok & up_ok, src.at[pl.ds(0, rows)], dst.at[pl.ds(base + height, rows)],
                   dt, -1, None if recv_ok is None else recv_ok & down_ok, slots[1])
        return low, high

    always = t >= 0
    slots = halos(not_last, guess, prev, depth, 1, always)
    halos(first, initial, prev, depth, 0, None, slots)
    for j, ref in enumerate((crow, ccol, diff)):
        halos(always, ref, raw.at[j], depth - 1, 0, always)
    for j in range(depth - 1):
        halos(always, forcing.at[j], frc.at[j], depth - 1 - j, 0, always)
    add(not_last, guess, prev.at[field], 1, 0, not_first)
    assert len(starts) == nstart
    for ok, copy, _ in starts:
        pl.when(ok)(copy.start)
    def coefficients(row, a, b, d):
        cu = jnp.maximum(a, 0.0) + d
        cd = d - jnp.minimum(a, 0.0)
        cl = jnp.maximum(b, 0.0) + d
        cr = d - jnp.minimum(b, 0.0)
        coef[0, row] = cu
        coef[1, row] = cd
        coef[2, row] = cl
        coef[3, row] = cr
        coef[4, row] = 1.0 - ((cu + cd) + (cl + cr))

    def local(i, carry):
        coefficients(base + i, crow[i], ccol[i], diff[i])
        for j in range(depth - 1):
            frc[j, base + i] = forcing[j, i]
        return carry

    lax.fori_loop(0, height, local, 0)

    @pl.when(first)
    def _():
        def body(i, carry):
            prev[base + i] = initial[i]
            return carry

        lax.fori_loop(0, height, body, 0)

    for _, copy, ok in starts:
        if ok is not None:
            pl.when(ok)(copy.wait_recv)

    edges = list(range(1, base)) + list(range(base + height, total - 1))
    for row in edges:
        coefficients(row, raw[0, row], raw[1, row], raw[2, row])

    def step(ext, row, count):
        rows = pl.ds(row, count)
        u = ext[1:-1]
        left, right = shifted(u)
        return (
            (coef[4, rows] * u + coef[0, rows] * ext[:-2])
            + (coef[1, rows] * ext[2:] + coef[2, rows] * left)
            + coef[3, rows] * right
        )

    def sweep(src, margin, finish):
        low = base - margin

        def body(i, carry):
            row = low + i * BLOCK
            finish(row, step(src[pl.ds(row - 1, BLOCK + 2)], row, BLOCK))
            return carry

        lax.fori_loop(0, (height + 2 * margin) // BLOCK, body, 0)

    def advance(src, dst, j, margin, keep=False):
        def finish(row, value):
            value = value + frc[j, pl.ds(row, BLOCK)]
            dst[pl.ds(row, BLOCK)] = value

        sweep(src, margin, finish)

    buffers = (wa, wb)
    src = prev
    for j in range(depth - 1):
        advance(src, buffers[j % 2], j, depth - 1 - j)
        src = buffers[j % 2]

    def residual(row, value):
        rows = pl.ds(row - base, BLOCK)
        res[rows] = value + forcing[depth - 1, rows] - guess[rows]

    sweep(src, 0, residual)

    halo = depth - 1

    def e_copies(i):
        low, high = i * PIECE, height - (i + 1) * PIECE
        copies = [
            (not_last, not_first, remote(eout.at[pl.ds(row, PIECE)], ein.at[pl.ds(base + row, PIECE)],
                                         esend.at[side, i], erecv.at[side, i], 1, 0))
            for side, row in ((0, low), (1, high))
        ]
        rows = min(halo - low, PIECE)
        if rows > 0:
            copies.append((not_last & up_ok, not_first & down_ok, remote(
                eout.at[pl.ds(low, rows)], ein.at[pl.ds(base + height + low, rows)],
                esend.at[2, i], erecv.at[2, i], 1, -1)))
            copies.append((not_last & down_ok, not_first & up_ok, remote(
                eout.at[pl.ds(height - low - rows, rows)], ein.at[pl.ds(base - low - rows, rows)],
                esend.at[3, i], erecv.at[3, i], 1, 1)))
        return copies

    def wait_e(i):
        for _, ok, copy in e_copies(i):
            pl.when(ok)(copy.wait_recv)

    def coarse(row):
        reach = depth // 2
        x = ein[pl.ds(base + row - reach, PIECE + 2 * reach)]
        for k in range(reach):
            size = x.shape[0] - 2
            x = 2.0 * step(x, base + row - reach + k + 1, size) - x[1:-1]
        rows = pl.ds(row, PIECE)
        e = x + res[rows]
        eout[rows] = e
        out[depth - 1, rows] = guess[rows] + e

    wait_e(0)
    for i in range(pieces):
        if i + 1 < pieces:
            wait_e(i + 1)
        coarse(i * PIECE)
        coarse(height - (i + 1) * PIECE)
        if i >= FLIGHT:
            for ok, _, copy in e_copies(i - FLIGHT):
                pl.when(ok)(copy.wait_send)
        for ok, _, copy in e_copies(i):
            pl.when(ok)(copy.start)

    def corrected(i, carry):
        wb[i + 1] = prev[i + 1] + ein[i + 1]
        return carry

    lax.fori_loop(0, total - 2, corrected, 0)
    src = wb
    for j in range(depth - 1):
        dst = buffers[j % 2]
        margin = depth - 2 - j

        def finish(row, value, j=j, dst=dst):
            value = value + frc[j, pl.ds(row, BLOCK)]
            out[j, pl.ds(row - base, BLOCK)] = value
            if j < depth - 2:
                dst[pl.ds(row, BLOCK)] = value

        sweep(src, 0, finish)
        if margin:
            for row in (base - margin, base + height):
                rows = pl.ds(row, margin)
                dst[rows] = step(src[pl.ds(row - 1, margin + 2)], row, margin) + frc[j, rows]
        src = dst

    for ok, copy, _ in starts:
        pl.when(ok)(copy.wait_send)
    for i in range(max(0, pieces - FLIGHT), pieces):
        for ok, _, copy in e_copies(i):
            pl.when(ok)(copy.wait_send)


def on_device(tcount, scount, guess, forcing, initial, crow, ccol, diff):
    depth, height, width = guess.shape
    lanes = width // SUB
    assert lanes % LANES == 0 and height % (2 * PIECE) == 0
    total = height + 2 * depth
    nstart = 2 * (2 + 3 + depth - 1) + 1
    f32 = jnp.float32
    dma = pltpu.SemaphoreType.DMA

    def rows_of(value):
        return value.reshape(value.shape[:-1] + (SUB, lanes))

    def buffer(*dims):
        return pltpu.VMEM(dims + (SUB, lanes), f32)

    states = pl.pallas_call(
        functools.partial(kernel, tcount, scount, depth, height, lanes, nstart),
        out_shape=jax.ShapeDtypeStruct((depth, height, SUB, lanes), f32),
        in_specs=[pl.BlockSpec(memory_space=pltpu.VMEM)] * 6,
        out_specs=pl.BlockSpec(memory_space=pltpu.VMEM),
        scratch_shapes=[
            buffer(total),
            buffer(depth - 1, total),
            buffer(3, total),
            buffer(5, total),
            buffer(total),
            buffer(height),
            buffer(height),
            buffer(total),
            buffer(total),
            dma((nstart,)),
            dma((nstart,)),
            dma((4, height // (2 * PIECE))),
            dma((4, height // (2 * PIECE))),
        ],
        compiler_params=pltpu.CompilerParams(
            collective_id=0, has_side_effects=True, vmem_limit_bytes=40 << 20
        ),
    )(*map(rows_of, (guess[depth - 1], forcing, initial, crow, ccol, diff)))
    return states.reshape(guess.shape)


def solution(mesh):
    return jax.shard_map(
        functools.partial(on_device, mesh.shape["tm"], mesh.shape["space"]),
        mesh=mesh,
        in_specs=(
            P("tm", "space", None),
            P("tm", "space", None),
            P("space", None),
            P("space", None),
            P("space", None),
            P("space", None),
        ),
        out_specs=P("tm", "space", None),
        check_vma=False,
    )
```

```python
import functools

import jax
import jax.numpy as jnp
from jax import lax
from jax.experimental import pallas as pl
from jax.experimental.pallas import tpu as pltpu
from jax.sharding import PartitionSpec as P

SUB = 8
LANES = 128
PIECE = 2
FLIGHT = 2
BLOCK = 8
MESH = pl.DeviceIdType.MESH


def shifted(x):
    lane = lax.broadcasted_iota(jnp.int32, x.shape[:2] + (LANES,), 2)
    size = x.shape[2]
    left = pltpu.roll(x, 1, 2)
    edge = left[:, :, :LANES]
    edge = jnp.where(lane == 0, pltpu.roll(edge, 1, 1), edge)
    left = jnp.concatenate([edge, left[:, :, LANES:]], axis=2)
    right = pltpu.roll(x, size - 1, 2)
    edge = right[:, :, size - LANES:]
    edge = jnp.where(lane == LANES - 1, pltpu.roll(edge, SUB - 1, 1), edge)
    right = jnp.concatenate([right[:, :, : size - LANES], edge], axis=2)
    return left, right


def kernel(
    tcount, scount, depth, height, lanes, nstart,
    guess, forcing, initial, crow, ccol, diff, out,
    prev, frc, raw, coef, ein, eout, res, *rest,
):
    levels = tuple(rest[: depth - 1])
    ssend, srecv, esend, erecv = rest[depth - 1:]
    t = lax.axis_index("tm")
    s = lax.axis_index("space")
    base = depth
    total = height + 2 * depth
    pieces = height // (2 * PIECE)
    up_ok, down_ok = s > 0, s < scount - 1
    first, not_first, not_last = t == 0, t > 0, t < tcount - 1
    field = pl.ds(base, height)

    def remote(src, dst, ssem, rsem, dt, ds):
        return pltpu.make_async_remote_copy(
            src_ref=src, dst_ref=dst, send_sem=ssem, recv_sem=rsem,
            device_id=(t + dt, s + ds), device_id_type=MESH,
        )

    barrier = pltpu.get_barrier_semaphore()
    count = 0
    for dt in (-1, 0, 1):
        for ds in (-1, 0, 1):
            if dt == 0 and ds == 0:
                continue
            ok = (t + dt >= 0) & (t + dt < tcount) & (s + ds >= 0) & (s + ds < scount)

            @pl.when(ok)
            def _(dt=dt, ds=ds):
                pl.semaphore_signal(barrier, inc=1, device_id=(t + dt, s + ds), device_id_type=MESH)

            count = count + ok.astype(jnp.int32)

    def clear(rows):
        zero = jnp.zeros((rows.size, SUB, lanes), jnp.float32)
        prev[rows] = zero
        ein[rows] = zero
        for j in range(depth - 1):
            frc[j, rows] = zero
        for j in range(3):
            raw[j, rows] = zero

    @pl.when(s == 0)
    def _():
        clear(pl.ds(0, depth))

    @pl.when(s == scount - 1)
    def _():
        clear(pl.ds(base + height, depth))

    @pl.when(first)
    def _():
        def body(i, carry):
            ein[i] = jnp.zeros((SUB, lanes), jnp.float32)
            return carry

        lax.fori_loop(0, total, body, 0)

    pl.semaphore_wait(barrier, count)

    starts = []

    def add(send_ok, src, dst, dt, ds, recv_ok, slot=None):
        n = len(starts)
        starts.append((send_ok, remote(src, dst, ssend.at[n], srecv.at[n if slot is None else slot], dt, ds), recv_ok))
        return n

    def halos(send_ok, src, dst, rows, dt, recv_ok, slots=(None, None)):
        low = add(send_ok & down_ok, src.at[pl.ds(height - rows, rows)], dst.at[pl.ds(base - rows, rows)],
                  dt, 1, None if recv_ok is None else recv_ok & up_ok, slots[0])
        high = add(send_ok & up_ok, src.at[pl.ds(0, rows)], dst.at[pl.ds(base + height, rows)],
                   dt, -1, None if recv_ok is None else recv_ok & down_ok, slots[1])
        return low, high

    always = t >= 0
    slots = halos(not_last, guess, prev, depth, 1, always)
    halos(first, initial, prev, depth, 0, None, slots)
    for j, ref in enumerate((crow, ccol, diff)):
        halos(always, ref, raw.at[j], depth - 1, 0, always)
    for j in range(depth - 1):
        halos(always, forcing.at[j], frc.at[j], depth - 1 - j, 0, always)
    add(not_last, guess, prev.at[field], 1, 0, not_first)
    assert len(starts) == nstart
    for ok, copy, _ in starts:
        pl.when(ok)(copy.start)
    def coefficients(row, a, b, d):
        cu = jnp.maximum(a, 0.0) + d
        cd = d - jnp.minimum(a, 0.0)
        cl = jnp.maximum(b, 0.0) + d
        cr = d - jnp.minimum(b, 0.0)
        coef[0, row] = cu
        coef[1, row] = cd
        coef[2, row] = cl
        coef[3, row] = cr
        coef[4, row] = 1.0 - ((cu + cd) + (cl + cr))

    def local(i, carry):
        coefficients(base + i, crow[i], ccol[i], diff[i])
        for j in range(depth - 1):
            frc[j, base + i] = forcing[j, i]
        return carry

    lax.fori_loop(0, height, local, 0)

    @pl.when(first)
    def _():
        def body(i, carry):
            prev[base + i] = initial[i]
            return carry

        lax.fori_loop(0, height, body, 0)

    pl.when(not_first)(starts[-1][1].wait_recv)

    def step(ext, row, count):
        rows = pl.ds(row, count)
        u = ext[1:-1]
        left, right = shifted(u)
        return (
            (coef[4, rows] * u + coef[0, rows] * ext[:-2])
            + (coef[1, rows] * ext[2:] + coef[2, rows] * left)
            + coef[3, rows] * right
        )

    def sweep(src, low, high, finish):
        def body(i, carry):
            row = jnp.minimum(low + i * BLOCK, high - BLOCK)
            finish(row, step(src[pl.ds(row - 1, BLOCK + 2)], row, BLOCK), BLOCK)
            return carry

        lax.fori_loop(0, -(-(high - low) // BLOCK), body, 0)

    fields = (prev,) + levels

    def relaxed(j):
        def finish(row, value, size):
            if j < depth - 1:
                rows = pl.ds(row, size)
                levels[j][rows] = value + frc[j, rows]
            else:
                rows = pl.ds(row - base, size)
                res[rows] = value + forcing[j, rows] - guess[rows]

        return finish

    for j in range(depth):
        sweep(fields[j], base + j + 1, base + height - j - 1, relaxed(j))
    for _, copy, ok in starts[:-1]:
        if ok is not None:
            pl.when(ok)(copy.wait_recv)
    edges = list(range(1, base)) + list(range(base + height, total - 1))
    for row in edges:
        coefficients(row, raw[0, row], raw[1, row], raw[2, row])
    for j in range(depth):
        for row in (base - depth + 1 + j, base + height - j - 1):
            relaxed(j)(row, step(fields[j][pl.ds(row - 1, depth + 2)], row, depth), depth)

    halo = depth - 1

    def e_copies(i):
        low, high = i * PIECE, height - (i + 1) * PIECE
        copies = [
            (not_last, not_first, remote(eout.at[pl.ds(row, PIECE)], ein.at[pl.ds(base + row, PIECE)],
                                         esend.at[side, i], erecv.at[side, i], 1, 0))
            for side, row in ((0, low), (1, high))
        ]
        rows = min(halo - low, PIECE)
        if rows > 0:
            copies.append((not_last & up_ok, not_first & down_ok, remote(
                eout.at[pl.ds(low, rows)], ein.at[pl.ds(base + height + low, rows)],
                esend.at[2, i], erecv.at[2, i], 1, -1)))
            copies.append((not_last & down_ok, not_first & up_ok, remote(
                eout.at[pl.ds(height - low - rows, rows)], ein.at[pl.ds(base - low - rows, rows)],
                esend.at[3, i], erecv.at[3, i], 1, 1)))
        return copies

    def wait_e(i):
        for _, ok, copy in e_copies(i):
            pl.when(ok)(copy.wait_recv)

    def coarse(row):
        reach = depth // 2
        x = ein[pl.ds(base + row - reach, PIECE + 2 * reach)]
        for k in range(reach):
            size = x.shape[0] - 2
            x = 2.0 * step(x, base + row - reach + k + 1, size) - x[1:-1]
        rows = pl.ds(row, PIECE)
        e = x + res[rows]
        eout[rows] = e
        out[depth - 1, rows] = guess[rows] + e

    wait_e(0)
    for i in range(pieces):
        if i + 1 < pieces:
            wait_e(i + 1)
        coarse(i * PIECE)
        coarse(height - (i + 1) * PIECE)
        if i >= FLIGHT:
            for ok, _, copy in e_copies(i - FLIGHT):
                pl.when(ok)(copy.wait_send)
        for ok, _, copy in e_copies(i):
            pl.when(ok)(copy.start)

    def corrected(i, carry):
        levels[-1][i + 1] = prev[i + 1] + ein[i + 1]
        return carry

    lax.fori_loop(0, total - 2, corrected, 0)
    src = levels[-1]
    for j in range(depth - 1):
        dst = levels[j % 2]
        margin = depth - 2 - j

        def finish(row, value, size, j=j, dst=dst):
            rows = pl.ds(row, size)
            value = value + frc[j, rows]
            out[j, pl.ds(row - base, size)] = value
            if j < depth - 2:
                dst[rows] = value

        sweep(src, base, base + height, finish)
        if margin:
            for row in (base - margin, base + height):
                rows = pl.ds(row, margin)
                dst[rows] = step(src[pl.ds(row - 1, margin + 2)], row, margin) + frc[j, rows]
        src = dst

    for ok, copy, _ in starts:
        pl.when(ok)(copy.wait_send)
    for i in range(max(0, pieces - FLIGHT), pieces):
        for ok, _, copy in e_copies(i):
            pl.when(ok)(copy.wait_send)


def on_device(tcount, scount, guess, forcing, initial, crow, ccol, diff):
    depth, height, width = guess.shape
    lanes = width // SUB
    assert lanes % LANES == 0 and height % (2 * PIECE) == 0
    total = height + 2 * depth
    nstart = 2 * (2 + 3 + depth - 1) + 1
    f32 = jnp.float32
    dma = pltpu.SemaphoreType.DMA

    def rows_of(value):
        return value.reshape(value.shape[:-1] + (SUB, lanes))

    def buffer(*dims):
        return pltpu.VMEM(dims + (SUB, lanes), f32)

    states = pl.pallas_call(
        functools.partial(kernel, tcount, scount, depth, height, lanes, nstart),
        out_shape=jax.ShapeDtypeStruct((depth, height, SUB, lanes), f32),
        in_specs=[pl.BlockSpec(memory_space=pltpu.VMEM)] * 6,
        out_specs=pl.BlockSpec(memory_space=pltpu.VMEM),
        scratch_shapes=[
            buffer(total),
            buffer(depth - 1, total),
            buffer(3, total),
            buffer(5, total),
            buffer(total),
            buffer(height),
            buffer(height),
            *[buffer(total) for _ in range(depth - 1)],
            dma((nstart,)),
            dma((nstart,)),
            dma((4, height // (2 * PIECE))),
            dma((4, height // (2 * PIECE))),
        ],
        compiler_params=pltpu.CompilerParams(
            collective_id=0, has_side_effects=True, vmem_limit_bytes=40 << 20
        ),
    )(*map(rows_of, (guess[depth - 1], forcing, initial, crow, ccol, diff)))
    return states.reshape(guess.shape)


def solution(mesh):
    return jax.shard_map(
        functools.partial(on_device, mesh.shape["tm"], mesh.shape["space"]),
        mesh=mesh,
        in_specs=(
            P("tm", "space", None),
            P("tm", "space", None),
            P("space", None),
            P("space", None),
            P("space", None),
            P("space", None),
        ),
        out_specs=P("tm", "space", None),
        check_vma=False,
    )
```

```python
import functools

import jax
import jax.numpy as jnp
from jax import lax
from jax.experimental import pallas as pl
from jax.experimental.pallas import tpu as pltpu
from jax.sharding import PartitionSpec as P

SUB = 8
LANES = 128
PIECE = 2
FLIGHT = 2
BLOCK = 8
MESH = pl.DeviceIdType.MESH


def shifted(x):
    lane = lax.broadcasted_iota(jnp.int32, x.shape[:2] + (LANES,), 2)
    size = x.shape[2]
    left = pltpu.roll(x, 1, 2)
    edge = left[:, :, :LANES]
    edge = jnp.where(lane == 0, pltpu.roll(edge, 1, 1), edge)
    left = jnp.concatenate([edge, left[:, :, LANES:]], axis=2)
    right = pltpu.roll(x, size - 1, 2)
    edge = right[:, :, size - LANES:]
    edge = jnp.where(lane == LANES - 1, pltpu.roll(edge, SUB - 1, 1), edge)
    right = jnp.concatenate([right[:, :, : size - LANES], edge], axis=2)
    return left, right


def kernel(
    tcount, scount, depth, height, lanes, nstart,
    guess, forcing, initial, crow, ccol, diff, out,
    prev, frc, raw, coef, ein, eout, res, *rest,
):
    levels = tuple(rest[: depth - 1])
    ssend, srecv, esend, erecv = rest[depth - 1:]
    t = lax.axis_index("tm")
    s = lax.axis_index("space")
    base = depth
    total = height + 2 * depth
    pieces = height // (2 * PIECE)
    up_ok, down_ok = s > 0, s < scount - 1
    first, not_first, not_last = t == 0, t > 0, t < tcount - 1
    field = pl.ds(base, height)

    def remote(src, dst, ssem, rsem, dt, ds):
        return pltpu.make_async_remote_copy(
            src_ref=src, dst_ref=dst, send_sem=ssem, recv_sem=rsem,
            device_id=(t + dt, s + ds), device_id_type=MESH,
        )

    barrier = pltpu.get_barrier_semaphore()
    count = 0
    for dt in (-1, 0, 1):
        for ds in (-1, 0, 1):
            if dt == 0 and ds == 0:
                continue
            ok = (t + dt >= 0) & (t + dt < tcount) & (s + ds >= 0) & (s + ds < scount)

            @pl.when(ok)
            def _(dt=dt, ds=ds):
                pl.semaphore_signal(barrier, inc=1, device_id=(t + dt, s + ds), device_id_type=MESH)

            count = count + ok.astype(jnp.int32)

    def clear(rows):
        zero = jnp.zeros((rows.size, SUB, lanes), jnp.float32)
        prev[rows] = zero
        ein[rows] = zero
        for j in range(depth - 1):
            frc[j, rows] = zero
        for j in range(3):
            raw[j, rows] = zero

    @pl.when(s == 0)
    def _():
        clear(pl.ds(0, depth))

    @pl.when(s == scount - 1)
    def _():
        clear(pl.ds(base + height, depth))

    @pl.when(first)
    def _():
        def body(i, carry):
            ein[i] = jnp.zeros((SUB, lanes), jnp.float32)
            return carry

        lax.fori_loop(0, total, body, 0)

    pl.semaphore_wait(barrier, count)

    starts = []

    def add(send_ok, src, dst, dt, ds, recv_ok, slot=None):
        n = len(starts)
        starts.append((send_ok, remote(src, dst, ssend.at[n], srecv.at[n if slot is None else slot], dt, ds), recv_ok))
        return n

    def halos(send_ok, src, dst, rows, dt, recv_ok, slots=(None, None)):
        low = add(send_ok & down_ok, src.at[pl.ds(height - rows, rows)], dst.at[pl.ds(base - rows, rows)],
                  dt, 1, None if recv_ok is None else recv_ok & up_ok, slots[0])
        high = add(send_ok & up_ok, src.at[pl.ds(0, rows)], dst.at[pl.ds(base + height, rows)],
                   dt, -1, None if recv_ok is None else recv_ok & down_ok, slots[1])
        return low, high

    always = t >= 0
    slots = halos(not_last, guess, prev, depth, 1, always)
    halos(first, initial, prev, depth, 0, None, slots)
    for j, ref in enumerate((crow, ccol, diff)):
        halos(always, ref, raw.at[j], depth - 1, 0, always)
    for j in range(depth - 1):
        halos(always, forcing.at[j], frc.at[j], depth - 1 - j, 0, always)
    add(not_last, guess, prev.at[field], 1, 0, not_first)
    assert len(starts) == nstart
    for ok, copy, _ in starts[-1:] + starts[2:-1] + starts[:2]:
        pl.when(ok)(copy.start)
    def coefficients(row, a, b, d):
        cu = jnp.maximum(a, 0.0) + d
        cd = d - jnp.minimum(a, 0.0)
        cl = jnp.maximum(b, 0.0) + d
        cr = d - jnp.minimum(b, 0.0)
        coef[0, row] = cu
        coef[1, row] = cd
        coef[2, row] = cl
        coef[3, row] = cr
        coef[4, row] = 1.0 - ((cu + cd) + (cl + cr))

    def local(i, carry):
        coefficients(base + i, crow[i], ccol[i], diff[i])
        for j in range(depth - 1):
            frc[j, base + i] = forcing[j, i]
        return carry

    lax.fori_loop(0, height, local, 0)

    @pl.when(first)
    def _():
        def body(i, carry):
            prev[base + i] = initial[i]
            return carry

        lax.fori_loop(0, height, body, 0)

    pl.when(not_first)(starts[-1][1].wait_recv)

    def step(ext, row, count):
        rows = pl.ds(row, count)
        u = ext[1:-1]
        left, right = shifted(u)
        return (
            (coef[4, rows] * u + coef[0, rows] * ext[:-2])
            + (coef[1, rows] * ext[2:] + coef[2, rows] * left)
            + coef[3, rows] * right
        )

    def sweep(src, low, high, finish):
        def body(i, carry):
            row = jnp.minimum(low + i * BLOCK, high - BLOCK)
            finish(row, step(src[pl.ds(row - 1, BLOCK + 2)], row, BLOCK), BLOCK)
            return carry

        lax.fori_loop(0, -(-(high - low) // BLOCK), body, 0)

    fields = (prev,) + levels

    def relaxed(j):
        def finish(row, value, size):
            if j < depth - 1:
                rows = pl.ds(row, size)
                levels[j][rows] = value + frc[j, rows]
            else:
                rows = pl.ds(row - base, size)
                res[rows] = value + forcing[j, rows] - guess[rows]

        return finish

    for j in range(depth):
        sweep(fields[j], base + j + 1, base + height - j - 1, relaxed(j))
    for _, copy, ok in starts[:-1]:
        if ok is not None:
            pl.when(ok)(copy.wait_recv)
    edges = list(range(1, base)) + list(range(base + height, total - 1))
    for row in edges:
        coefficients(row, raw[0, row], raw[1, row], raw[2, row])
    for j in range(depth):
        for row in (base - depth + 1 + j, base + height - j - 1):
            relaxed(j)(row, step(fields[j][pl.ds(row - 1, depth + 2)], row, depth), depth)

    halo = depth - 1

    def e_copies(i):
        low, high = i * PIECE, height - (i + 1) * PIECE
        copies = [
            (not_last, not_first, remote(eout.at[pl.ds(row, PIECE)], ein.at[pl.ds(base + row, PIECE)],
                                         esend.at[side, i], erecv.at[side, i], 1, 0))
            for side, row in ((0, low), (1, high))
        ]
        rows = min(halo - low, PIECE)
        if rows > 0:
            copies.append((not_last & up_ok, not_first & down_ok, remote(
                eout.at[pl.ds(low, rows)], ein.at[pl.ds(base + height + low, rows)],
                esend.at[2, i], erecv.at[2, i], 1, -1)))
            copies.append((not_last & down_ok, not_first & up_ok, remote(
                eout.at[pl.ds(height - low - rows, rows)], ein.at[pl.ds(base - low - rows, rows)],
                esend.at[3, i], erecv.at[3, i], 1, 1)))
        return copies[2:] + copies[:2]

    def wait_e(i):
        for _, ok, copy in e_copies(i):
            pl.when(ok)(copy.wait_recv)

    def coarse(row):
        reach = depth // 2
        x = ein[pl.ds(base + row - reach, PIECE + 2 * reach)]
        for k in range(reach):
            size = x.shape[0] - 2
            x = 2.0 * step(x, base + row - reach + k + 1, size) - x[1:-1]
        rows = pl.ds(row, PIECE)
        e = x + res[rows]
        eout[rows] = e
        out[depth - 1, rows] = guess[rows] + e

    ahead = -(-(depth // 2) // PIECE)
    for i in range(ahead):
        wait_e(i)
    for i in range(pieces):
        if i + ahead < pieces:
            wait_e(i + ahead)
        coarse(i * PIECE)
        coarse(height - (i + 1) * PIECE)
        if i >= FLIGHT:
            for ok, _, copy in e_copies(i - FLIGHT):
                pl.when(ok)(copy.wait_send)
        for ok, _, copy in e_copies(i):
            pl.when(ok)(copy.start)

    def corrected(i, carry):
        levels[-1][i + 1] = prev[i + 1] + ein[i + 1]
        return carry

    lax.fori_loop(0, total - 2, corrected, 0)
    src = levels[-1]
    for j in range(depth - 1):
        dst = levels[j % 2]
        margin = depth - 2 - j

        def finish(row, value, size, j=j, dst=dst):
            rows = pl.ds(row, size)
            value = value + frc[j, rows]
            out[j, pl.ds(row - base, size)] = value
            if j < depth - 2:
                dst[rows] = value

        sweep(src, base, base + height, finish)
        if margin:
            for row in (base - margin, base + height):
                rows = pl.ds(row, margin)
                dst[rows] = step(src[pl.ds(row - 1, margin + 2)], row, margin) + frc[j, rows]
        src = dst

    for ok, copy, _ in starts:
        pl.when(ok)(copy.wait_send)
    for i in range(max(0, pieces - FLIGHT), pieces):
        for ok, _, copy in e_copies(i):
            pl.when(ok)(copy.wait_send)


def on_device(tcount, scount, guess, forcing, initial, crow, ccol, diff):
    depth, height, width = guess.shape
    lanes = width // SUB
    assert lanes % LANES == 0 and height % (2 * PIECE) == 0
    total = height + 2 * depth
    nstart = 2 * (2 + 3 + depth - 1) + 1
    f32 = jnp.float32
    dma = pltpu.SemaphoreType.DMA

    def rows_of(value):
        return value.reshape(value.shape[:-1] + (SUB, lanes))

    def buffer(*dims):
        return pltpu.VMEM(dims + (SUB, lanes), f32)

    states = pl.pallas_call(
        functools.partial(kernel, tcount, scount, depth, height, lanes, nstart),
        out_shape=jax.ShapeDtypeStruct((depth, height, SUB, lanes), f32),
        in_specs=[pl.BlockSpec(memory_space=pltpu.VMEM)] * 6,
        out_specs=pl.BlockSpec(memory_space=pltpu.VMEM),
        scratch_shapes=[
            buffer(total),
            buffer(depth - 1, total),
            buffer(3, total),
            buffer(5, total),
            buffer(total),
            buffer(height),
            buffer(height),
            *[buffer(total) for _ in range(depth - 1)],
            dma((nstart,)),
            dma((nstart,)),
            dma((4, height // (2 * PIECE))),
            dma((4, height // (2 * PIECE))),
        ],
        compiler_params=pltpu.CompilerParams(
            collective_id=0, has_side_effects=True, vmem_limit_bytes=40 << 20
        ),
    )(*map(rows_of, (guess[depth - 1], forcing, initial, crow, ccol, diff)))
    return states.reshape(guess.shape)


def solution(mesh):
    return jax.shard_map(
        functools.partial(on_device, mesh.shape["tm"], mesh.shape["space"]),
        mesh=mesh,
        in_specs=(
            P("tm", "space", None),
            P("tm", "space", None),
            P("space", None),
            P("space", None),
            P("space", None),
            P("space", None),
        ),
        out_specs=P("tm", "space", None),
        check_vma=False,
    )
```
